32 devices in a mesh: row: 8 (over y, x, core), col: 4 (over z).
Axes of the slice: x: 2, y: 2, z: 4, core: 2. Of those that a mesh axis runs over, the one named last changes fastest.
Arguments:
- density: bfloat16 [4096, 4096], P('row', 'col'), as said below
- pattern: int32 [64, 64], P('row', 'col'), may hold values from 0 to 1, as said below
Outputs:
- updated: bfloat16 [4096, 4096], P('row', 'col')
- occupations: float32 [2], replicated
The draws below stay inside these ranges and needn't reach their ends.
Inputs may be any that keep to these rules, and one draw needn't show every extreme that they name: pattern is symmetric, every diagonal block is 1. density is exactly symmetric and zero wherever pattern is 0.
All inputs are finite; a program needn't handle non-finite values.
Results may differ from the reference program's by a relative error of at most 0.0015.
Values may be sent and summed in bfloat16 or wider, within the bound.
A program may use at most 64 MiB of HBM per device.

```python
import math
import jax
import jax.numpy as jnp

BLK = 64
NB = 64
ORDER = 4096


def pattern_of(key):
    draws_int = jax.random.randint(jax.random.fold_in(key, 7), (NB, NB), 0, 5)
    diagonal_mask = jnp.arange(NB)[:, None] == jnp.arange(NB)[None, :]
    kept_blocks = (draws_int < 2) | (draws_int.T < 2) | diagonal_mask
    return kept_blocks.astype(jnp.int32)


def draw_pattern(key, part):
    return pattern_of(key)


def draw_density(key, part):
    kept_blocks = pattern_of(key).astype(jnp.float32)
    cell_mask = jnp.broadcast_to(kept_blocks[:, None, :, None], (NB, BLK, NB, BLK)).reshape(ORDER, ORDER)
    position = jnp.arange(ORDER).astype(jnp.float32)
    key_entries = jax.random.fold_in(key, 11)
    key_rough = jax.random.fold_in(key, 12)
    key_diag = jax.random.fold_in(key, 13)
    entries = jax.random.normal(key_entries, (ORDER, ORDER), jnp.float32)
    roughness = jnp.exp(jax.random.uniform(key_rough, (ORDER,), jnp.float32, 0.0, math.log(10.0 / 3.0)))
    row_scale = jnp.sqrt(jnp.exp(math.log(3.0) * position / ORDER) * roughness)
    outer_scale = row_scale[:, None] * row_scale[None, :]
    symmetric = (entries + entries.T) * 0.70710678
    coefficient = (0.64 * ORDER * 21.5) ** (-0.25)
    diag_values = jax.random.uniform(key_diag, (ORDER,), jnp.float32, 0.5, 1.5) * row_scale * row_scale
    dense = cell_mask * symmetric * outer_scale * coefficient + jnp.diag(diag_values)
    return dense.astype(jnp.bfloat16)


def setup_inputs(seed: int = 0) -> dict:
    key_list = jax.random.split(jax.random.key(seed), 3)
    return {
        "density": draw_density(jax.random.fold_in(key_list[2], 71), 0),
        "pattern": draw_pattern(jax.random.fold_in(key_list[2], 71), 0),
    }


def expand_blocks(block_mask, width):
    block_rows, block_cols = block_mask.shape
    grid = jnp.broadcast_to(block_mask.astype(jnp.float32)[:, None, :, None], (block_rows, width, block_cols, width))
    return grid.reshape(block_rows * width, block_cols * width)


def reference(density, pattern):
    cell_mask = expand_blocks(pattern, BLK)
    square = jnp.dot(density, density, preferred_element_type=jnp.float32) * cell_mask
    density_wide = density.astype(jnp.float32)
    trace_p = jnp.sum(jnp.diagonal(density_wide))
    trace_c = jnp.sum(jnp.diagonal(square))
    take_square = trace_p > 1.0 * ORDER
    updated = jnp.where(take_square, square, cell_mask * (2.0 * density_wide - square))
    trace_new = jnp.where(take_square, trace_c, 2.0 * trace_p - trace_c)
    occupations = jnp.stack([trace_p, trace_new]) / ORDER
    return updated.astype(jnp.bfloat16), occupations.astype(jnp.float32)
```

```python
import functools

import jax
import jax.numpy as jnp
from jax import lax
from jax.experimental import pallas as pl
from jax.experimental.pallas import tpu as pltpu
from jax.sharding import PartitionSpec as P

BLK = 64
MESH = pl.DeviceIdType.MESH
NCH = 4


def expand_blocks(block_mask, width):
    block_rows, block_cols = block_mask.shape
    grid = jnp.broadcast_to(
        block_mask.astype(jnp.float32)[:, None, :, None], (block_rows, width, block_cols, width)
    )
    return grid.reshape(block_rows * width, block_cols * width)


def plain_body(density, pattern):
    slab_rows, slab_cols = density.shape
    cell_mask = expand_blocks(pattern, BLK)
    column_panel = lax.all_gather(density, "row", axis=0, tiled=True)
    row_offset = lax.axis_index("row") * slab_rows
    col_offset = lax.axis_index("col") * slab_cols
    global_rows = row_offset + lax.iota(jnp.int32, slab_rows)
    global_cols = col_offset + lax.iota(jnp.int32, slab_cols)
    on_diagonal = global_rows[:, None] == global_cols[None, :]
    density_wide = density.astype(jnp.float32)
    trace_p_part = jnp.sum(jnp.where(on_diagonal, density_wide, 0.0))
    square = jnp.dot(
        lax.all_gather(density, "col", axis=1, tiled=True),
        column_panel,
        preferred_element_type=jnp.float32,
    )
    square = square * cell_mask
    trace_c_part = jnp.sum(jnp.where(on_diagonal, square, 0.0))
    trace_p, trace_c = lax.psum((trace_p_part, trace_c_part), ("row", "col"))
    order_total = slab_rows * lax.axis_size("row")
    take_square = trace_p > 1.0 * order_total
    updated = jnp.where(take_square, square, cell_mask * (2.0 * density_wide - square))
    trace_new = jnp.where(take_square, trace_c, 2.0 * trace_p - trace_c)
    occupations = jnp.stack([trace_p, trace_new]) / order_total
    return (updated.astype(jnp.bfloat16), occupations)


def kernel(order_total, p_ref, pat_ref, out_ref, occ_ref, arow, bcol, acc, tz, tp, tsum,
           up_s, up_r, dn_s, dn_r, x_s, x_r, y_s, y_r, s_s, s_r, tz_s, tz_r, tp_s, tp_r):
    rows, cols = p_ref.shape
    ch = rows // NCH
    r = lax.axis_index("row")
    c = lax.axis_index("col")
    core = r % 2
    x = (r // 2) % 2
    y = r // 4
    sib = r + 1 - 2 * core
    xn = r + 2 - 4 * x
    yn = r + 4 - 8 * y
    dg = xn + 4 - 8 * y

    barrier = pltpu.get_barrier_semaphore()
    for d in range(1, 8):
        pl.semaphore_signal(barrier, inc=1, device_id=((r + d) % 8, c), device_id_type=MESH)
    for d in range(1, 4):
        pl.semaphore_signal(barrier, inc=1, device_id=(r, (c + d) % 4), device_id_type=MESH)
    pl.semaphore_wait(barrier, 10)

    def send(src, dst, ss, rs, dev):
        return pltpu.make_async_remote_copy(
            src_ref=src, dst_ref=dst, send_sem=ss, recv_sem=rs, device_id=dev, device_id_type=MESH
        )

    def piece(k):
        return pl.ds(k * ch, ch) if isinstance(k, int) else pl.ds(pl.multiple_of(k * ch, ch), ch)

    def z_up(slot, own, k):
        src = p_ref if own else arow.at[slot]
        pos = k
        return send(src.at[piece(k % NCH)], arow.at[slot, piece(k % NCH)],
                    up_s.at[pos], up_r.at[pos], (r, (c + 1) % 4))

    def z_dn(slot, own, k):
        src = p_ref if own else arow.at[slot]
        return send(src.at[piece(k % NCH)], arow.at[slot, piece(k % NCH)],
                    dn_s.at[k], dn_r.at[k], (r, (c + 3) % 4))

    def x_own(k):
        return send(p_ref.at[piece(k)], bcol.at[r, piece(k)], x_s.at[k], x_r.at[k], (xn, c))

    def y_own(k):
        return send(p_ref.at[piece(k)], bcol.at[r, piece(k)], y_s.at[k], y_r.at[k], (yn, c))

    def y_fwd(k):
        return send(bcol.at[xn, piece(k)], bcol.at[xn, piece(k)], y_s.at[4 + k], y_r.at[4 + k], (yn, c))

    def x_fwd(k):
        return send(bcol.at[yn, piece(k)], bcol.at[yn, piece(k)], x_s.at[2 + k], x_r.at[2 + k], (xn, c))

    def sib_fwd(slot, k, pos, own=False):
        src = p_ref if own else bcol.at[slot]
        return send(src.at[piece(k)], bcol.at[slot, piece(k)], s_s.at[pos], s_r.at[pos], (sib, c))

    def got(ref, sem):
        send(ref, ref, sem, sem, (sib, c)).wait_recv()

    for k in range(NCH):
        @pl.when(c < 3)
        def _(k=k):
            z_up(c, True, k).start()

        @pl.when(c > 0)
        def _(k=k):
            z_dn(c, True, k).start()

        x_own(k).start()
        y_own((k + 2) % NCH).start()
    for k in range(NCH):
        sib_fwd(r, k, k, True).start()

    def part(i, carry):
        tpp, tcc = carry
        start = pl.multiple_of(i * 64, 64)
        v = p_ref[pl.ds(start, 64), :]
        arow[c, pl.ds(start, 64), :] = v
        bcol[r, pl.ds(start, 64), :] = v
        w = v.astype(jnp.float32)
        gr = lax.broadcasted_iota(jnp.int32, w.shape, 0) + (r * rows + start)
        gc = lax.broadcasted_iota(jnp.int32, w.shape, 1) + c * cols
        dpart = jnp.where(gr == gc, w, 0.0)
        return tpp + jnp.sum(dpart, axis=0, keepdims=True), tcc + jnp.sum(w * w, axis=0, keepdims=True)

    zero = jnp.zeros((1, cols), jnp.float32)
    tpp, tcc = lax.fori_loop(0, rows // 64, part, (zero, zero))
    which = lax.broadcasted_iota(jnp.int32, (8, 128), 0)
    tz[c] = jnp.where(which == 0, jnp.sum(tpp), jnp.sum(tcc))
    tz_out = [send(tz.at[c], tz.at[c], tz_s.at[d], tz_r.at[d], (r, (c + d) % 4)) for d in range(1, 4)]
    for t in tz_out:
        t.start()

    def z_step(i):
        @pl.when(i < NCH * c)
        def _():
            slot = c - 1 - i // NCH
            got(arow.at[slot, piece(i % NCH)], up_r.at[i])

            @pl.when(c < 3)
            def _():
                k = i + NCH
                send(arow.at[slot, piece(i % NCH)], arow.at[slot, piece(i % NCH)],
                     up_s.at[k], up_r.at[k], (r, (c + 1) % 4)).start()

        @pl.when(i < NCH * (3 - c))
        def _():
            slot = c + 1 + i // NCH
            got(arow.at[slot, piece(i % NCH)], dn_r.at[i])

            @pl.when(c > 0)
            def _():
                k = i + NCH
                send(arow.at[slot, piece(i % NCH)], arow.at[slot, piece(i % NCH)],
                     dn_s.at[k], dn_r.at[k], (r, (c + 3) % 4)).start()

    for i in range(6):
        if i < 4:
            kx, ky = i, (i + 2) % NCH
            got(bcol.at[xn, piece(kx)], x_r.at[kx])
            if kx < 2:
                y_fwd(kx).start()
            sib_fwd(xn, kx, 4 + kx).start()
            got(bcol.at[yn, piece(ky)], y_r.at[ky])
            if ky >= 2:
                x_fwd(ky).start()
            sib_fwd(yn, ky, 8 + ky).start()
        else:
            k = i - 4
            got(bcol.at[dg, piece(2 + k)], x_r.at[4 + k])
            sib_fwd(dg, 2 + k, 14 + k).start()
            got(bcol.at[dg, piece(k)], y_r.at[4 + k])
            sib_fwd(dg, k, 12 + k).start()
        z_step(i)
        if i == 1:
            for t in tz_out:
                t.wait_send()
            for d in range(1, 4):
                got(tz.at[(c + 4 - d) % 4], tz_r.at[d])
            tp[r] = ((tz[0] + tz[1]) + tz[2]) + tz[3]
            tp_out = [send(tp.at[r], tp.at[r], tp_s.at[d], tp_r.at[d], ((r + d) % 8, c)) for d in range(1, 8)]
            for t in tp_out:
                t.start()

    sr = sib
    sx, sy, sd = xn + 1 - 2 * core, yn + 1 - 2 * core, dg + 1 - 2 * core
    for slot, base in ((sr, 0), (sx, 4), (sy, 8), (sd, 12)):
        for k in range(NCH):
            got(bcol.at[slot, piece(k)], s_r.at[base + k])
    z_step(6)

    def mm(slot, k, first=False):
        rr = piece(k)
        a = arow[slot, rr, :]
        half = cols // 2
        v = jnp.dot(a[:, :half], bcol[2 * slot], preferred_element_type=jnp.float32)
        v += jnp.dot(a[:, half:], bcol[2 * slot + 1], preferred_element_type=jnp.float32)
        acc[rr, :] = v if first else acc[rr, :] + v

    def own_mm(k, _):
        mm(c, k, True)
        return 0

    lax.fori_loop(0, NCH, own_mm, 0)
    z_step(7)

    def near(i, _):
        @pl.when(i < NCH * c)
        def _():
            mm(c - 1 - i // NCH, i % NCH)

        @pl.when(i < NCH * (3 - c))
        def _():
            mm(c + 1 + i // NCH, i % NCH)
        return 0

    def tail(i, _):
        z_step(i)
        near(i - NCH, 0)
        return 0

    lax.fori_loop(0, NCH, near, 0)
    lax.fori_loop(2 * NCH, 3 * NCH, tail, 0)
    lax.fori_loop(2 * NCH, 3 * NCH, near, 0)

    for t in tp_out:
        t.wait_send()
    for d in range(1, 8):
        got(tp.at[(r + 8 - d) % 8], tp_r.at[d])
    tot = tp[0]
    for d in range(1, 8):
        tot = tot + tp[d]
    tsum[...] = tot
    sel = lax.broadcasted_iota(jnp.int32, (8, 128), 1) == 0
    trace_p = jnp.sum(jnp.where(sel & (which == 0), tot, 0.0))
    trace_c = jnp.sum(jnp.where(sel & (which == 1), tot, 0.0))
    take = trace_p > 1.0 * order_total
    occ_ref[0] = trace_p / order_total
    occ_ref[1] = jnp.where(take, trace_c, 2.0 * trace_p - trace_c) / order_total
    takev = tsum[0:1, 0:1] > 1.0 * order_total

    nbr, nbc = pat_ref.shape
    spread = (lax.broadcasted_iota(jnp.int32, (nbc, cols), 1) // BLK
              == lax.broadcasted_iota(jnp.int32, (nbc, cols), 0)).astype(jnp.float32)
    mask = jnp.dot(pat_ref[...].astype(jnp.float32), spread, preferred_element_type=jnp.float32)
    for b in range(nbr):
        rr = pl.ds(b * BLK, BLK)
        m = mask[b:b + 1, :]
        sq = acc[rr, :] * m
        alt = m * (2.0 * p_ref[rr, :].astype(jnp.float32) - sq)
        out_ref[rr, :] = jnp.where(takev, sq, alt).astype(jnp.bfloat16)

    for k in range(NCH):
        x_own(k).wait_send()
        y_own(k).wait_send()
    for k in range(2):
        y_fwd(k).wait_send()
        x_fwd(2 + k).wait_send()
    for pos in range(16):
        sib_fwd(r, 0, pos, True).wait_send()
    for i in range(4 * NCH - 4):
        @pl.when((c < 3) & (i < NCH * (c + 1)))
        def _(i=i):
            z_up(c, True, i).wait_send()

        @pl.when((c > 0) & (i < NCH * (4 - c)))
        def _(i=i):
            z_dn(c, True, i).wait_send()


def body(density, pattern):
    rows, cols = density.shape
    order_total = rows * lax.axis_size("row")
    dma = pltpu.SemaphoreType.DMA
    return pl.pallas_call(
        functools.partial(kernel, order_total),
        out_shape=(jax.ShapeDtypeStruct((rows, cols), jnp.bfloat16),
                   jax.ShapeDtypeStruct((2,), jnp.float32)),
        in_specs=[pl.BlockSpec(memory_space=pltpu.VMEM)] * 2,
        out_specs=(pl.BlockSpec(memory_space=pltpu.VMEM), pl.BlockSpec(memory_space=pltpu.SMEM)),
        scratch_shapes=[
            pltpu.VMEM((4, rows, cols), jnp.bfloat16),
            pltpu.VMEM((8, rows, cols), jnp.bfloat16),
            pltpu.VMEM((rows, cols), jnp.float32),
            pltpu.VMEM((4, 8, 128), jnp.float32),
            pltpu.VMEM((8, 8, 128), jnp.float32),
            pltpu.VMEM((8, 128), jnp.float32),
            dma((12,)), dma((12,)), dma((12,)), dma((12,)),
            dma((6,)), dma((6,)), dma((6,)), dma((6,)),
            dma((16,)), dma((16,)),
            dma((4,)), dma((4,)), dma((8,)), dma((8,)),
        ],
        compiler_params=pltpu.CompilerParams(
            collective_id=0, has_side_effects=True, vmem_limit_bytes=40 * 2**20
        ),
    )(density, pattern)


def solution(mesh):
    placed = (P("row", "col"), P("row", "col"))
    fits = mesh.shape["row"] == 8 and mesh.shape["col"] == 4
    return jax.shard_map(
        body if fits else plain_body, mesh=mesh, in_specs=placed,
        out_specs=(P("row", "col"), P()), check_vma=False
    )
```

```python
import functools

import jax
import jax.numpy as jnp
from jax import lax
from jax.experimental import pallas as pl
from jax.experimental.pallas import tpu as pltpu
from jax.sharding import PartitionSpec as P

BLK = 64
MESH = pl.DeviceIdType.MESH
NCH = 4


def expand_blocks(block_mask, width):
    block_rows, block_cols = block_mask.shape
    grid = jnp.broadcast_to(
        block_mask.astype(jnp.float32)[:, None, :, None], (block_rows, width, block_cols, width)
    )
    return grid.reshape(block_rows * width, block_cols * width)


def plain_body(density, pattern):
    slab_rows, slab_cols = density.shape
    cell_mask = expand_blocks(pattern, BLK)
    column_panel = lax.all_gather(density, "row", axis=0, tiled=True)
    row_offset = lax.axis_index("row") * slab_rows
    col_offset = lax.axis_index("col") * slab_cols
    global_rows = row_offset + lax.iota(jnp.int32, slab_rows)
    global_cols = col_offset + lax.iota(jnp.int32, slab_cols)
    on_diagonal = global_rows[:, None] == global_cols[None, :]
    density_wide = density.astype(jnp.float32)
    trace_p_part = jnp.sum(jnp.where(on_diagonal, density_wide, 0.0))
    square = jnp.dot(
        lax.all_gather(density, "col", axis=1, tiled=True),
        column_panel,
        preferred_element_type=jnp.float32,
    )
    square = square * cell_mask
    trace_c_part = jnp.sum(jnp.where(on_diagonal, square, 0.0))
    trace_p, trace_c = lax.psum((trace_p_part, trace_c_part), ("row", "col"))
    order_total = slab_rows * lax.axis_size("row")
    take_square = trace_p > 1.0 * order_total
    updated = jnp.where(take_square, square, cell_mask * (2.0 * density_wide - square))
    trace_new = jnp.where(take_square, trace_c, 2.0 * trace_p - trace_c)
    occupations = jnp.stack([trace_p, trace_new]) / order_total
    return (updated.astype(jnp.bfloat16), occupations)


def kernel(order_total, p_ref, pat_ref, out_ref, occ_ref, arow, bcol, acc, xa, xb, tz, tp, tsum,
           mid_s, mid_r, inn_s, inn_r, edge_s, edge_r, dia_s, xa_r, xb_r, fa_s, fb_s,
           x_s, x_r, y_s, y_r, s_s, s_r, tz_s, tz_r, tp_s, tp_r):
    rows, cols = p_ref.shape
    ch = rows // NCH
    half = cols // 2
    r = lax.axis_index("row")
    c = lax.axis_index("col")
    core = r % 2
    x = (r // 2) % 2
    y = r // 4
    sib = r + 1 - 2 * core
    xn = r + 2 - 4 * x
    yn = r + 4 - 8 * y
    dg = xn + 4 - 8 * y
    flip = c // 2
    chip = r // 2
    role = chip + flip * (3 - 2 * chip)
    is_mid = (c == 1) | (c == 2)
    is_end = (c == 0) | (c == 3)
    inward = (c + 1 - 2 * flip) % 4
    outward = (c + 3 + 2 * flip) % 4
    zhalf = jnp.where(role == 3, core, 1 - core)

    def blk(b):
        return b + flip * (3 - 2 * b)

    barrier = pltpu.get_barrier_semaphore()
    for d in range(1, 8):
        pl.semaphore_signal(barrier, inc=1, device_id=((r + d) % 8, c), device_id_type=MESH)
    for d in range(1, 4):
        pl.semaphore_signal(barrier, inc=1, device_id=(r, (c + d) % 4), device_id_type=MESH)
    pl.semaphore_wait(barrier, 10)

    def send(src, dst, ss, rs, dev):
        return pltpu.make_async_remote_copy(
            src_ref=src, dst_ref=dst, send_sem=ss, recv_sem=rs, device_id=dev, device_id_type=MESH
        )

    def got(ref, sem):
        send(ref, ref, sem, sem, (sib, c)).wait_recv()

    def start(t):
        t.start()

    def drain(t):
        t.wait_send()

    def piece(k):
        return pl.ds(k * ch, ch) if isinstance(k, int) else pl.ds(pl.multiple_of(k * ch, ch), ch)

    def lane(h):
        return pl.ds(pl.multiple_of(h * half, half), half)

    def inn(k):
        return send(p_ref.at[piece(k)], arow.at[c, piece(k)], inn_s.at[k], inn_r.at[k], (r, inward))

    def mid(pos):
        src = p_ref if pos < NCH else arow.at[blk(0)]
        slot = blk(1) if pos < NCH else blk(0)
        k = pos % NCH
        return send(src.at[piece(k)], arow.at[slot, piece(k)], mid_s.at[pos], mid_r.at[pos], (r, inward))

    def edge(d, k, act):
        pos = (d - 1) * NCH + k
        src = p_ref if d == 1 else arow.at[blk(d)]

        @pl.when(role == d)
        def _():
            act(send(src.at[piece(k)], arow.at[blk(d), piece(k)],
                     edge_s.at[pos], edge_r.at[pos], (r, outward)))

        @pl.when((role != d) & (role != 0))
        def _():
            act(send(src.at[piece(k), lane(zhalf)], arow.at[blk(d), piece(k), lane(zhalf)],
                     edge_s.at[pos], edge_r.at[pos], (r, outward)))

    def edge_got(d, k):
        pos = (d - 1) * NCH + k

        @pl.when(role == d)
        def _():
            got(arow.at[blk(d), piece(k)], edge_r.at[pos])

        @pl.when((role != d) & (role != 0))
        def _():
            got(arow.at[blk(d), piece(k), lane(zhalf)], edge_r.at[pos])

        if d < 3:
            @pl.when(role == 3)
            def _():
                share_far(d, k).start()
        else:
            @pl.when(role == 1)
            def _():
                share_near(1, k).start()

            @pl.when(role == 2)
            def _():
                share_near(2, k).start()

    def share_far(d, k):
        sem = (fa_s if d == 1 else fb_s).at[k]
        return send(arow.at[blk(d), piece(k), lane(zhalf)], xb.at[piece(k)], sem, xb_r.at[k],
                    (yn if d == 1 else xn, c))

    def share_near(me, k):
        dst, sem = (xa, xa_r) if me == 1 else (xb, xb_r)
        to = (yn if me == 1 else xn) + 1 - 2 * core
        return send(arow.at[blk(3), piece(k), lane(zhalf)], dst.at[piece(k)], fa_s.at[k], sem.at[k], (to, c))

    def dia(k):
        return send(bcol.at[yn, piece(k), lane(core)], xa.at[piece(k)], dia_s.at[k], xa_r.at[k], (r, outward))

    def dia_x(k):
        return send(xa.at[piece(k)], xa.at[piece(k)], fa_s.at[k], xa_r.at[k], (xn, c))

    def dia_y(k):
        return send(xa.at[piece(k)], xa.at[piece(k)], fb_s.at[k], xa_r.at[k], (yn, c))

    def x_own(k):
        return send(p_ref.at[piece(k)], bcol.at[r, piece(k)], x_s.at[k], x_r.at[k], (xn, c))

    def y_own(k):
        return send(p_ref.at[piece(k)], bcol.at[r, piece(k)], y_s.at[k], y_r.at[k], (yn, c))

    def y_fwd(k):
        return send(bcol.at[xn, piece(k)], bcol.at[xn, piece(k)], y_s.at[4 + k], y_r.at[4 + k], (yn, c))

    def x_fwd(k):
        return send(bcol.at[yn, piece(k)], bcol.at[yn, piece(k)], x_s.at[2 + k], x_r.at[2 + k], (xn, c))

    def sib_fwd(slot, k, pos, own=False):
        src = p_ref if own else bcol.at[slot]
        return send(src.at[piece(k)], bcol.at[slot, piece(k)], s_s.at[pos], s_r.at[pos], (sib, c))

    for k in range(NCH):
        @pl.when(is_end)
        def _(k=k):
            inn(k).start()

        @pl.when(is_mid)
        def _(k=k):
            mid(k).start()
            edge(1, k, start)

        x_own(k).start()
        y_own((k + 2) % NCH).start()
    for k in range(NCH):
        sib_fwd(r, k, k, True).start()

    def part(i, carry):
        tpp, tcc = carry
        at = pl.multiple_of(i * 64, 64)
        v = p_ref[pl.ds(at, 64), :]
        arow[c, pl.ds(at, 64), :] = v
        bcol[r, pl.ds(at, 64), :] = v
        w = v.astype(jnp.float32)
        gr = lax.broadcasted_iota(jnp.int32, w.shape, 0) + (r * rows + at)
        gc = lax.broadcasted_iota(jnp.int32, w.shape, 1) + c * cols
        dpart = jnp.where(gr == gc, w, 0.0)
        return tpp + jnp.sum(dpart, axis=0, keepdims=True), tcc + jnp.sum(w * w, axis=0, keepdims=True)

    zero = jnp.zeros((1, cols), jnp.float32)
    tpp, tcc = lax.fori_loop(0, rows // 64, part, (zero, zero))
    which = lax.broadcasted_iota(jnp.int32, (8, 128), 0)
    tz[c] = jnp.where(which == 0, jnp.sum(tpp), jnp.sum(tcc))
    tz_out = [send(tz.at[c], tz.at[c], tz_s.at[d], tz_r.at[d], (r, (c + d) % 4)) for d in range(1, 4)]
    for t in tz_out:
        t.start()
    tp_out = [send(tp.at[r], tp.at[r], tp_s.at[d], tp_r.at[d], ((r + d) % 8, c)) for d in range(1, 8)]

    def mid_step(i):
        if i < NCH:
            got(arow.at[blk(0), piece(i)], inn_r.at[i])
            mid(NCH + i).start()
        b = 2 + i // NCH
        got(arow.at[blk(b), piece(i % NCH)], mid_r.at[i])
        edge(b, i % NCH, start)

    for i in range(6):
        if i < 4:
            kx, ky = i, (i + 2) % NCH
            got(bcol.at[xn, piece(kx)], x_r.at[kx])
            if kx < 2:
                y_fwd(kx).start()
            sib_fwd(xn, kx, 4 + kx).start()
            got(bcol.at[yn, piece(ky)], y_r.at[ky])
            if ky >= 2:
                x_fwd(ky).start()
            sib_fwd(yn, ky, 8 + ky).start()

            @pl.when(is_mid & (role == 0))
            def _():
                dia(ky).start()
        else:
            k = i - 4
            got(bcol.at[dg, piece(2 + k)], x_r.at[4 + k])
            sib_fwd(dg, 2 + k, 14 + k).start()
            got(bcol.at[dg, piece(k)], y_r.at[4 + k])
            sib_fwd(dg, k, 12 + k).start()

        @pl.when(is_mid)
        def _():
            mid_step(i)

        @pl.when(is_end)
        def _():
            edge_got(1 + i // NCH, i % NCH)

        if i >= 1 and i < 5:
            kd = (i + 1) % NCH

            @pl.when(is_end & (role == 0))
            def _():
                got(xa.at[piece(kd)], xa_r.at[kd])
                dia_x(kd).start()
                dia_y(kd).start()
        if i == 1:
            for t in tz_out:
                t.wait_send()
            for d in range(1, 4):
                got(tz.at[(c + 4 - d) % 4], tz_r.at[d])
            tp[r] = ((tz[0] + tz[1]) + tz[2]) + tz[3]
            for t in tp_out:
                t.start()

    sx, sy, sd = xn + 1 - 2 * core, yn + 1 - 2 * core, dg + 1 - 2 * core
    for slot, base in ((sib, 0), (sx, 4), (sy, 8), (sd, 12)):
        for k in range(NCH):
            got(bcol.at[slot, piece(k)], s_r.at[base + k])

    def mm(b, h, first=False):
        slot = blk(b)

        def some(k, _):
            rr = piece(k)
            v = jnp.dot(arow[slot, rr, lane(h)], bcol[2 * slot + h], preferred_element_type=jnp.float32)
            acc[rr, :] = v if first else acc[rr, :] + v
            return 0

        lax.fori_loop(0, NCH, some, 0)

    def mm_all(b):
        lax.fori_loop(0, 2, lambda h, _: (mm(b, h), 0)[1], 0)

    def turn(src, b, h):
        for k in range(NCH):
            arow[blk(b), :, pl.ds(pl.multiple_of(h * half + k * ch, ch), ch)] = src(k).T

    @pl.when(is_mid)
    def _():
        mid_step(6)
        mm(1, 0, True)
        mm(1, 1)
        mid_step(7)
        mm_all(0)
        mm_all(2)
        mm_all(3)

    @pl.when(is_end)
    def _():
        edge_got(2, 2)
        mm(0, 0, True)
        mm(0, 1)
        edge_got(2, 3)

        @pl.when(role == 0)
        def _():
            def slab(t, _):
                b, h = 1 + t // 2, t % 2
                turn(lambda k: bcol[2 * blk(b) + h, piece(k), lane(core)], b, h)
                mm(b, h)
                return 0

            lax.fori_loop(0, 6, slab, 0)

        def all_xa():
            for k in range(NCH):
                got(xa.at[piece(k)], xa_r.at[k])

        def all_xb():
            for k in range(NCH):
                got(xb.at[piece(k)], xb_r.at[k])

        other = 1 - zhalf

        @pl.when(role == 1)
        def _():
            all_xa()
            turn(lambda k: xa[piece(k), :], 2, other)
            all_xb()
            turn(lambda k: xb[piece(k), :], 3, other)

        @pl.when(role == 2)
        def _():
            all_xa()
            arow[blk(1), :, lane(other)] = xa[...]
            all_xb()
            turn(lambda k: xb[piece(k), :], 3, other)

        @pl.when((role == 1) | (role == 2))
        def _():
            mm_all(1)
            edge_got(3, 0)
            mm_all(2)
            edge_got(3, 1)
            mm(3, other)
            edge_got(3, 2)
            edge_got(3, 3)
            mm(3, zhalf)

        @pl.when(role == 3)
        def _():
            mm(1, zhalf)
            mm(2, zhalf)
            for k in range(NCH):
                edge_got(3, k)
            mm_all(3)
            all_xa()
            turn(lambda k: xa[piece(k), :], 1, other)
            mm(1, other)
            all_xb()
            turn(lambda k: xb[piece(k), :], 2, other)
            mm(2, other)

    for t in tp_out:
        t.wait_send()
    for d in range(1, 8):
        got(tp.at[(r + 8 - d) % 8], tp_r.at[d])
    tot = tp[0]
    for d in range(1, 8):
        tot = tot + tp[d]
    tsum[...] = tot
    sel = lax.broadcasted_iota(jnp.int32, (8, 128), 1) == 0
    trace_p = jnp.sum(jnp.where(sel & (which == 0), tot, 0.0))
    trace_c = jnp.sum(jnp.where(sel & (which == 1), tot, 0.0))
    take = trace_p > 1.0 * order_total
    occ_ref[0] = trace_p / order_total
    occ_ref[1] = jnp.where(take, trace_c, 2.0 * trace_p - trace_c) / order_total
    takev = tsum[0:1, 0:1] > 1.0 * order_total

    nbr, nbc = pat_ref.shape
    spread = (lax.broadcasted_iota(jnp.int32, (nbc, cols), 1) // BLK
              == lax.broadcasted_iota(jnp.int32, (nbc, cols), 0)).astype(jnp.float32)
    mask = jnp.dot(pat_ref[...].astype(jnp.float32), spread, preferred_element_type=jnp.float32)
    for b in range(nbr):
        rr = pl.ds(b * BLK, BLK)
        m = mask[b:b + 1, :]
        sq = acc[rr, :] * m
        alt = m * (2.0 * p_ref[rr, :].astype(jnp.float32) - sq)
        out_ref[rr, :] = jnp.where(takev, sq, alt).astype(jnp.bfloat16)

    for k in range(NCH):
        x_own(k).wait_send()
        y_own(k).wait_send()
    for k in range(2):
        y_fwd(k).wait_send()
        x_fwd(2 + k).wait_send()
    for pos in range(16):
        sib_fwd(r, 0, pos, True).wait_send()

    @pl.when(is_mid)
    def _():
        for pos in range(2 * NCH):
            mid(pos).wait_send()
        for d in range(1, 4):
            for k in range(NCH):
                edge(d, k, drain)

        @pl.when(role == 0)
        def _():
            for k in range(NCH):
                dia(k).wait_send()

    @pl.when(is_end)
    def _():
        for k in range(NCH):
            inn(k).wait_send()

        @pl.when(role == 0)
        def _():
            for k in range(NCH):
                dia_x(k).wait_send()
                dia_y(k).wait_send()

        @pl.when(role == 3)
        def _():
            for k in range(NCH):
                share_far(1, k).wait_send()
                share_far(2, k).wait_send()

        @pl.when((role == 1) | (role == 2))
        def _():
            for k in range(NCH):
                share_near(1, k).wait_send()


def body(density, pattern):
    rows, cols = density.shape
    order_total = rows * lax.axis_size("row")
    dma = pltpu.SemaphoreType.DMA
    return pl.pallas_call(
        functools.partial(kernel, order_total),
        out_shape=(jax.ShapeDtypeStruct((rows, cols), jnp.bfloat16),
                   jax.ShapeDtypeStruct((2,), jnp.float32)),
        in_specs=[pl.BlockSpec(memory_space=pltpu.VMEM)] * 2,
        out_specs=(pl.BlockSpec(memory_space=pltpu.VMEM), pl.BlockSpec(memory_space=pltpu.SMEM)),
        scratch_shapes=[
            pltpu.VMEM((4, rows, cols), jnp.bfloat16),
            pltpu.VMEM((8, rows, cols), jnp.bfloat16),
            pltpu.VMEM((rows, cols), jnp.float32),
            pltpu.VMEM((rows, cols // 2), jnp.bfloat16),
            pltpu.VMEM((rows, cols // 2), jnp.bfloat16),
            pltpu.VMEM((4, 8, 128), jnp.float32),
            pltpu.VMEM((8, 8, 128), jnp.float32),
            pltpu.VMEM((8, 128), jnp.float32),
            dma((8,)), dma((8,)), dma((4,)), dma((4,)), dma((12,)), dma((12,)),
            dma((4,)), dma((4,)), dma((4,)), dma((4,)), dma((4,)),
            dma((6,)), dma((6,)), dma((6,)), dma((6,)),
            dma((16,)), dma((16,)),
            dma((4,)), dma((4,)), dma((8,)), dma((8,)),
        ],
        compiler_params=pltpu.CompilerParams(
            collective_id=0, has_side_effects=True, vmem_limit_bytes=40 * 2**20
        ),
    )(density, pattern)


def solution(mesh):
    placed = (P("row", "col"), P("row", "col"))
    fits = mesh.shape["row"] == 8 and mesh.shape["col"] == 4
    return jax.shard_map(
        body if fits else plain_body, mesh=mesh, in_specs=placed,
        out_specs=(P("row", "col"), P()), check_vma=False
    )
```

```python
import functools

import jax
import jax.numpy as jnp
from jax import lax
from jax.experimental import pallas as pl
from jax.experimental.pallas import tpu as pltpu
from jax.sharding import PartitionSpec as P

BLK = 64
MESH = pl.DeviceIdType.MESH
NCH = 4
HALF = NCH // 2


def expand_blocks(block_mask, width):
    block_rows, block_cols = block_mask.shape
    grid = jnp.broadcast_to(
        block_mask.astype(jnp.float32)[:, None, :, None], (block_rows, width, block_cols, width)
    )
    return grid.reshape(block_rows * width, block_cols * width)


def plain_body(density, pattern):
    slab_rows, slab_cols = density.shape
    cell_mask = expand_blocks(pattern, BLK)
    column_panel = lax.all_gather(density, "row", axis=0, tiled=True)
    row_offset = lax.axis_index("row") * slab_rows
    col_offset = lax.axis_index("col") * slab_cols
    global_rows = row_offset + lax.iota(jnp.int32, slab_rows)
    global_cols = col_offset + lax.iota(jnp.int32, slab_cols)
    on_diagonal = global_rows[:, None] == global_cols[None, :]
    density_wide = density.astype(jnp.float32)
    trace_p_part = jnp.sum(jnp.where(on_diagonal, density_wide, 0.0))
    square = jnp.dot(
        lax.all_gather(density, "col", axis=1, tiled=True),
        column_panel,
        preferred_element_type=jnp.float32,
    )
    square = square * cell_mask
    trace_c_part = jnp.sum(jnp.where(on_diagonal, square, 0.0))
    trace_p, trace_c = lax.psum((trace_p_part, trace_c_part), ("row", "col"))
    order_total = slab_rows * lax.axis_size("row")
    take_square = trace_p > 1.0 * order_total
    updated = jnp.where(take_square, square, cell_mask * (2.0 * density_wide - square))
    trace_new = jnp.where(take_square, trace_c, 2.0 * trace_p - trace_c)
    occupations = jnp.stack([trace_p, trace_new]) / order_total
    return (updated.astype(jnp.bfloat16), occupations)


def kernel(order_total, p_ref, pat_hbm, out_ref, occ_ref, arow, bcol, acc, xa, xb, tz, tp, tsum, pat_ref, mask, in_s,
           mid_s, mid_r, inn_s, inn_r, edge_s, edge_r, dia_s, xa_r, xb_r, fa_s, fb_s,
           x_s, x_r, y_s, y_r, s_s, s_r, tz_s, tz_r, tp_s, tp_r):
    rows, cols = p_ref.shape
    ch = rows // NCH
    mrows = 128
    half = cols // 2
    r = lax.axis_index("row")
    c = lax.axis_index("col")
    core = r % 2
    x = (r // 2) % 2
    y = r // 4
    sib = r + 1 - 2 * core
    xn = r + 2 - 4 * x
    yn = r + 4 - 8 * y
    dg = xn + 4 - 8 * y
    flip = c // 2
    chip = r // 2
    role = chip + flip * (3 - 2 * chip)
    is_mid = (c == 1) | (c == 2)
    is_end = (c == 0) | (c == 3)
    inward = (c + 1 - 2 * flip) % 4
    outward = (c + 3 + 2 * flip) % 4
    zhalf = jnp.where(role == 3, core, 1 - core)

    def blk(b):
        return b + flip * (3 - 2 * b)

    own_in = pltpu.make_async_copy(p_ref, arow.at[c], in_s.at[0])
    own_in.start()
    own_b = pltpu.make_async_copy(p_ref, bcol.at[r], in_s.at[1])
    own_b.start()
    pat_in = pltpu.make_async_copy(pat_hbm, pat_ref, in_s.at[2])
    pat_in.start()

    barrier = pltpu.get_barrier_semaphore()
    for d in range(1, 8):
        pl.semaphore_signal(barrier, inc=1, device_id=((r + d) % 8, c), device_id_type=MESH)
    for d in range(1, 4):
        pl.semaphore_signal(barrier, inc=1, device_id=(r, (c + d) % 4), device_id_type=MESH)
    pl.semaphore_wait(barrier, 10)

    def send(src, dst, ss, rs, dev):
        return pltpu.make_async_remote_copy(
            src_ref=src, dst_ref=dst, send_sem=ss, recv_sem=rs, device_id=dev, device_id_type=MESH
        )

    def got(ref, sem):
        send(ref, ref, sem, sem, (sib, c)).wait_recv()

    def start(t):
        t.start()

    def drain(t):
        t.wait_send()

    def piece(k):
        return pl.ds(k * ch, ch) if isinstance(k, int) else pl.ds(pl.multiple_of(k * ch, ch), ch)

    def lane(h):
        return pl.ds(pl.multiple_of(h * half, half), half)

    def inn(k):
        return send(p_ref.at[piece(k)], arow.at[c, piece(k)], inn_s.at[k], inn_r.at[k], (r, inward))

    def mid(pos):
        src = p_ref if pos < NCH else arow.at[blk(0)]
        slot = blk(1) if pos < NCH else blk(0)
        k = pos % NCH
        return send(src.at[piece(k)], arow.at[slot, piece(k)], mid_s.at[pos], mid_r.at[pos], (r, inward))

    def edge(d, k, act):
        pos = (d - 1) * NCH + k
        src = p_ref if d == 1 else arow.at[blk(d)]

        @pl.when(role == d)
        def _():
            act(send(src.at[piece(k)], arow.at[blk(d), piece(k)],
                     edge_s.at[pos], edge_r.at[pos], (r, outward)))

        @pl.when((role != d) & (role != 0))
        def _():
            act(send(src.at[piece(k), lane(zhalf)], arow.at[blk(d), piece(k), lane(zhalf)],
                     edge_s.at[pos], edge_r.at[pos], (r, outward)))

    def edge_got(d, k):
        pos = (d - 1) * NCH + k

        @pl.when(role == d)
        def _():
            got(arow.at[blk(d), piece(k)], edge_r.at[pos])

        @pl.when((role != d) & (role != 0))
        def _():
            got(arow.at[blk(d), piece(k), lane(zhalf)], edge_r.at[pos])

        if d < 3:
            @pl.when(role == 3)
            def _():
                share_far(d, k).start()
        else:
            @pl.when(role == 1)
            def _():
                share_near(1, k).start()

            @pl.when(role == 2)
            def _():
                share_near(2, k).start()

    def share_far(d, k):
        sem = (fa_s if d == 1 else fb_s).at[k]
        return send(arow.at[blk(d), piece(k), lane(zhalf)], xb.at[piece(k)], sem, xb_r.at[k],
                    (yn if d == 1 else xn, c))

    def share_near(me, k):
        dst, sem = (xa, xa_r) if me == 1 else (xb, xb_r)
        to = (yn if me == 1 else xn) + 1 - 2 * core
        return send(arow.at[blk(3), piece(k), lane(zhalf)], dst.at[piece(k)], fa_s.at[k], sem.at[k], (to, c))

    def dia(k):
        return send(bcol.at[yn, piece(k), lane(core)], xa.at[piece(k)], dia_s.at[k], xa_r.at[k], (r, outward))

    def dia_x(k):
        return send(xa.at[piece(k)], xa.at[piece(k)], fa_s.at[k], xa_r.at[k], (xn, c))

    def dia_y(k):
        return send(xa.at[piece(k)], xa.at[piece(k)], fb_s.at[k], xa_r.at[k], (yn, c))

    def x_own(k):
        return send(p_ref.at[piece(k)], bcol.at[r, piece(k)], x_s.at[k], x_r.at[k], (xn, c))

    def y_own(k):
        return send(p_ref.at[piece(k)], bcol.at[r, piece(k)], y_s.at[k], y_r.at[k], (yn, c))

    def y_fwd(k):
        return send(bcol.at[xn, piece(k)], bcol.at[xn, piece(k)], y_s.at[NCH + k], y_r.at[NCH + k], (yn, c))

    def x_fwd(k):
        return send(bcol.at[yn, piece(k)], bcol.at[yn, piece(k)], x_s.at[HALF + k], x_r.at[HALF + k], (xn, c))

    def sib_fwd(slot, k, pos, own=False):
        src = p_ref if own else bcol.at[slot]
        return send(src.at[piece(k)], bcol.at[slot, piece(k)], s_s.at[pos], s_r.at[pos], (sib, c))

    for k in range(NCH):
        @pl.when(is_end)
        def _(k=k):
            inn(k).start()

        @pl.when(is_mid)
        def _(k=k):
            mid(k).start()
            edge(1, k, start)

        x_own(k).start()
        y_own((k + HALF) % NCH).start()
    for k in range(NCH):
        sib_fwd(r, k, k, True).start()

    def part(i, carry):
        tpp, tcc = carry
        at = pl.multiple_of(i * 64, 64)
        w = arow[c, pl.ds(at, 64), :].astype(jnp.float32)
        gr = lax.broadcasted_iota(jnp.int32, w.shape, 0) + (r * rows + at)
        gc = lax.broadcasted_iota(jnp.int32, w.shape, 1) + c * cols
        dpart = jnp.where(gr == gc, w, 0.0)
        return tpp + jnp.sum(dpart, axis=0, keepdims=True), tcc + jnp.sum(w * w, axis=0, keepdims=True)

    own_in.wait()
    own_b.wait()
    pat_in.wait()
    zero = jnp.zeros((1, cols), jnp.float32)
    tpp, tcc = lax.fori_loop(0, rows // 64, part, (zero, zero))
    which = lax.broadcasted_iota(jnp.int32, (8, 128), 0)
    tz[c] = jnp.where(which == 0, jnp.sum(tpp), jnp.sum(tcc))
    tz_out = [send(tz.at[c], tz.at[c], tz_s.at[d], tz_r.at[d], (r, (c + d) % 4)) for d in range(1, 4)]
    for t in tz_out:
        t.start()
    tp_out = [send(tp.at[r], tp.at[r], tp_s.at[d], tp_r.at[d], ((r + d) % 8, c)) for d in range(1, 8)]

    def mid_step(i):
        if i < NCH:
            got(arow.at[blk(0), piece(i)], inn_r.at[i])
            mid(NCH + i).start()
        b = 2 + i // NCH
        got(arow.at[blk(b), piece(i % NCH)], mid_r.at[i])
        edge(b, i % NCH, start)

    for i in range(NCH + HALF):
        if i < NCH:
            kx, ky = i, (i + HALF) % NCH
            got(bcol.at[xn, piece(kx)], x_r.at[kx])
            if kx < HALF:
                y_fwd(kx).start()
            sib_fwd(xn, kx, NCH + kx).start()
            got(bcol.at[yn, piece(ky)], y_r.at[ky])
            if ky >= HALF:
                x_fwd(ky).start()
            sib_fwd(yn, ky, 2 * NCH + ky).start()

            @pl.when(is_mid & (role == 0))
            def _():
                dia(ky).start()
        else:
            k = i - NCH
            got(bcol.at[dg, piece(HALF + k)], x_r.at[NCH + k])
            sib_fwd(dg, HALF + k, 3 * NCH + HALF + k).start()
            got(bcol.at[dg, piece(k)], y_r.at[NCH + k])
            sib_fwd(dg, k, 3 * NCH + k).start()

        @pl.when(is_mid)
        def _():
            mid_step(i)

        @pl.when(is_end)
        def _():
            edge_got(1 + i // NCH, i % NCH)

        if i >= 1 and i <= NCH:
            kd = (i - 1 + HALF) % NCH

            @pl.when(is_end & (role == 0))
            def _():
                got(xa.at[piece(kd)], xa_r.at[kd])
                dia_x(kd).start()
                dia_y(kd).start()

    def traces():
        for d in range(1, 4):
            got(tz.at[(c + 4 - d) % 4], tz_r.at[d])
        tp[r] = ((tz[0] + tz[1]) + tz[2]) + tz[3]
        for t in tp_out:
            t.start()

    sx, sy, sd = xn + 1 - 2 * core, yn + 1 - 2 * core, dg + 1 - 2 * core
    for slot, base in ((sib, 0), (sx, NCH), (sy, 2 * NCH), (sd, 3 * NCH)):
        for k in range(NCH):
            got(bcol.at[slot, piece(k)], s_r.at[base + k])

    def mm(b, h, first=False, only=None):
        slot = blk(b)

        def some(k, _):
            rr = pl.ds(k * mrows, mrows) if isinstance(k, int) else pl.ds(pl.multiple_of(k * mrows, mrows), mrows)
            v = jnp.dot(arow[slot, rr, lane(h)], bcol[2 * slot + h], preferred_element_type=jnp.float32)
            acc[rr, :] = v if first else acc[rr, :] + v
            return 0

        if only is None:
            lax.fori_loop(0, rows // mrows, some, 0)
        else:
            some(only, 0)

    def totals():
        for d in range(1, 8):
            got(tp.at[(r + 8 - d) % 8], tp_r.at[d])
        tot = tp[0]
        for d in range(1, 8):
            tot = tot + tp[d]
        tsum[...] = tot
        sel = lax.broadcasted_iota(jnp.int32, (8, 128), 1) == 0
        trace_p = jnp.sum(jnp.where(sel & (which == 0), tot, 0.0))
        trace_c = jnp.sum(jnp.where(sel & (which == 1), tot, 0.0))
        take = trace_p > 1.0 * order_total
        occ_ref[0] = trace_p / order_total
        occ_ref[1] = jnp.where(take, trace_c, 2.0 * trace_p - trace_c) / order_total

    def mm_all(b):
        lax.fori_loop(0, 2, lambda h, _: (mm(b, h), 0)[1], 0)

    def turn(src, b, h):
        for k in range(NCH):
            arow[blk(b), :, pl.ds(pl.multiple_of(h * half + k * ch, ch), ch)] = src(k).T

    nbr, nbc = pat_ref.shape
    spread = (lax.broadcasted_iota(jnp.int32, (nbc, cols), 1) // BLK
              == lax.broadcasted_iota(jnp.int32, (nbc, cols), 0)).astype(jnp.float32)
    mask[...] = jnp.dot(pat_ref[...].astype(jnp.float32), spread, preferred_element_type=jnp.float32)

    @pl.when(is_mid)
    def _():
        for i in range(NCH + HALF, 2 * NCH - 1):
            mid_step(i)
        mm(1, 0, True)
        mm(1, 1)
        mm_all(0)
        traces()
        mid_step(2 * NCH - 1)
        totals()
        mm_all(2)
        mm_all(3)

    @pl.when(is_end)
    def _():
        mm(0, 0, True)
        mm(0, 1)
        for k in range(HALF, NCH):
            edge_got(2, k)
        traces()

        @pl.when(role == 0)
        def _():
            def slab(t, _):
                b, h = 1 + t // 2, t % 2
                turn(lambda k: bcol[2 * blk(b) + h, piece(k), lane(core)], b, h)
                mm(b, h)
                return 0

            lax.fori_loop(0, 6, slab, 0)
            totals()

        def all_xa():
            for k in range(NCH):
                got(xa.at[piece(k)], xa_r.at[k])

        def all_xb():
            for k in range(NCH):
                got(xb.at[piece(k)], xb_r.at[k])

        other = 1 - zhalf

        @pl.when(role == 1)
        def _():
            all_xa()
            turn(lambda k: xa[piece(k), :], 2, other)
            all_xb()
            turn(lambda k: xb[piece(k), :], 3, other)

        @pl.when(role == 2)
        def _():
            all_xa()
            arow[blk(1), :, lane(other)] = xa[...]
            all_xb()
            turn(lambda k: xb[piece(k), :], 3, other)

        per = mrows // ch

        @pl.when((role == 1) | (role == 2))
        def _():
            mm_all(1)
            mm(3, other)
            for k in range(HALF):
                edge_got(3, k)
            mm(2, 0)
            for k in range(HALF, NCH - 1):
                edge_got(3, k)
            mm(2, 1)
            totals()
            for k in range(3):
                mm(3, zhalf, only=k)
            edge_got(3, NCH - 1)
            mm(3, zhalf, only=3)

        def mm_part(b, h, src, sem, g):
            deep = half // 2
            for k in range(g * HALF, (g + 1) * HALF):
                got(src.at[piece(k)], sem.at[k])
            v = src[pl.ds(g * deep, deep), :].T
            slot = blk(b)
            depth = pl.ds(g * deep, deep)

            for m in range(rows // mrows):
                rr = pl.ds(m * mrows, mrows)
                acc[rr, :] += jnp.dot(v[m * mrows:(m + 1) * mrows, :], bcol[2 * slot + h, depth, :],
                                      preferred_element_type=jnp.float32)

        @pl.when(role == 3)
        def _():
            mm(1, zhalf)
            mm(2, zhalf)
            for k in range(NCH):
                edge_got(3, k)
                if (k + 1) % per == 0:
                    mm(3, 0, only=k // per)
                    mm(3, 1, only=k // per)
                if k == NCH - 2:
                    mm_part(1, other, xa, xa_r, 0)
                    mm_part(2, other, xb, xb_r, 0)
                    totals()
            mm_part(1, other, xa, xa_r, 1)
            mm_part(2, other, xb, xb_r, 1)

    takev = tsum[0:1, 0:1] > 1.0 * order_total
    for b in range(nbr):
        rr = pl.ds(b * BLK, BLK)
        m = mask[b:b + 1, :]
        sq = acc[rr, :] * m
        alt = m * (2.0 * arow[c, rr, :].astype(jnp.float32) - sq)
        out_ref[rr, :] = jnp.where(takev, sq, alt).astype(jnp.bfloat16)

    for t in tz_out + tp_out:
        t.wait_send()
    for k in range(NCH):
        x_own(k).wait_send()
        y_own(k).wait_send()
    for k in range(HALF):
        y_fwd(k).wait_send()
        x_fwd(HALF + k).wait_send()
    for pos in range(4 * NCH):
        sib_fwd(r, 0, pos, True).wait_send()

    @pl.when(is_mid)
    def _():
        for pos in range(2 * NCH):
            mid(pos).wait_send()
        for d in range(1, 4):
            for k in range(NCH):
                edge(d, k, drain)

        @pl.when(role == 0)
        def _():
            for k in range(NCH):
                dia(k).wait_send()

    @pl.when(is_end)
    def _():
        for k in range(NCH):
            inn(k).wait_send()

        @pl.when(role == 0)
        def _():
            for k in range(NCH):
                dia_x(k).wait_send()
                dia_y(k).wait_send()

        @pl.when(role == 3)
        def _():
            for k in range(NCH):
                share_far(1, k).wait_send()
                share_far(2, k).wait_send()

        @pl.when((role == 1) | (role == 2))
        def _():
            for k in range(NCH):
                share_near(1, k).wait_send()


def body(density, pattern):
    rows, cols = density.shape
    order_total = rows * lax.axis_size("row")
    dma = pltpu.SemaphoreType.DMA
    return pl.pallas_call(
        functools.partial(kernel, order_total),
        out_shape=(jax.ShapeDtypeStruct((rows, cols), jnp.bfloat16),
                   jax.ShapeDtypeStruct((2,), jnp.float32)),
        in_specs=[pl.BlockSpec(memory_space=pltpu.HBM)] * 2,
        out_specs=(pl.BlockSpec(memory_space=pltpu.VMEM), pl.BlockSpec(memory_space=pltpu.SMEM)),
        scratch_shapes=[
            pltpu.VMEM((4, rows, cols), jnp.bfloat16),
            pltpu.VMEM((8, rows, cols), jnp.bfloat16),
            pltpu.VMEM((rows, cols), jnp.float32),
            pltpu.VMEM((rows, cols // 2), jnp.bfloat16),
            pltpu.VMEM((rows, cols // 2), jnp.bfloat16),
            pltpu.VMEM((4, 8, 128), jnp.float32),
            pltpu.VMEM((8, 8, 128), jnp.float32),
            pltpu.VMEM((8, 128), jnp.float32),
            pltpu.VMEM(pattern.shape, jnp.int32),
            pltpu.VMEM((pattern.shape[0], cols), jnp.float32),
            dma((3,)),
            dma((2 * NCH,)), dma((2 * NCH,)), dma((NCH,)), dma((NCH,)), dma((3 * NCH,)), dma((3 * NCH,)),
            dma((NCH,)), dma((NCH,)), dma((NCH,)), dma((NCH,)), dma((NCH,)),
            dma((NCH + HALF,)), dma((NCH + HALF,)), dma((NCH + HALF,)), dma((NCH + HALF,)),
            dma((4 * NCH,)), dma((4 * NCH,)),
            dma((4,)), dma((4,)), dma((8,)), dma((8,)),
        ],
        compiler_params=pltpu.CompilerParams(
            collective_id=0, has_side_effects=True, vmem_limit_bytes=40 * 2**20
        ),
    )(density, pattern)


def solution(mesh):
    placed = (P("row", "col"), P("row", "col"))
    fits = mesh.shape["row"] == 8 and mesh.shape["col"] == 4
    return jax.shard_map(
        body if fits else plain_body, mesh=mesh, in_specs=placed,
        out_specs=(P("row", "col"), P()), check_vma=False
    )
```

```python
import functools

import jax
import jax.numpy as jnp
from jax import lax
from jax.experimental import pallas as pl
from jax.experimental.pallas import tpu as pltpu
from jax.sharding import PartitionSpec as P

BLK = 64
MESH = pl.DeviceIdType.MESH
NCH = 4
HALF = NCH // 2


def expand_blocks(block_mask, width):
    block_rows, block_cols = block_mask.shape
    grid = jnp.broadcast_to(
        block_mask.astype(jnp.float32)[:, None, :, None], (block_rows, width, block_cols, width)
    )
    return grid.reshape(block_rows * width, block_cols * width)


def plain_body(density, pattern):
    slab_rows, slab_cols = density.shape
    cell_mask = expand_blocks(pattern, BLK)
    column_panel = lax.all_gather(density, "row", axis=0, tiled=True)
    row_offset = lax.axis_index("row") * slab_rows
    col_offset = lax.axis_index("col") * slab_cols
    global_rows = row_offset + lax.iota(jnp.int32, slab_rows)
    global_cols = col_offset + lax.iota(jnp.int32, slab_cols)
    on_diagonal = global_rows[:, None] == global_cols[None, :]
    density_wide = density.astype(jnp.float32)
    trace_p_part = jnp.sum(jnp.where(on_diagonal, density_wide, 0.0))
    square = jnp.dot(
        lax.all_gather(density, "col", axis=1, tiled=True),
        column_panel,
        preferred_element_type=jnp.float32,
    )
    square = square * cell_mask
    trace_c_part = jnp.sum(jnp.where(on_diagonal, square, 0.0))
    trace_p, trace_c = lax.psum((trace_p_part, trace_c_part), ("row", "col"))
    order_total = slab_rows * lax.axis_size("row")
    take_square = trace_p > 1.0 * order_total
    updated = jnp.where(take_square, square, cell_mask * (2.0 * density_wide - square))
    trace_new = jnp.where(take_square, trace_c, 2.0 * trace_p - trace_c)
    occupations = jnp.stack([trace_p, trace_new]) / order_total
    return (updated.astype(jnp.bfloat16), occupations)


def kernel(order_total, p_ref, pat_hbm, out_ref, occ_ref, arow, bcol, acc, xa, xb, tz, tp, tsum, pat_ref, mask, in_s,
           mid_s, mid_r, inn_s, inn_r, edge_s, edge_r, dia_s, xa_r, xb_r, fa_s, fb_s,
           x_s, x_r, y_s, y_r, s_s, s_r, tz_s, tz_r, tp_s, tp_r):
    rows, cols = p_ref.shape
    ch = rows // NCH
    mrows = 128
    half = cols // 2
    r = lax.axis_index("row")
    c = lax.axis_index("col")
    core = r % 2
    x = (r // 2) % 2
    y = r // 4
    sib = r + 1 - 2 * core
    xn = r + 2 - 4 * x
    yn = r + 4 - 8 * y
    dg = xn + 4 - 8 * y
    flip = c // 2
    chip = r // 2
    role = chip + flip * (3 - 2 * chip)
    is_mid = (c == 1) | (c == 2)
    is_end = (c == 0) | (c == 3)
    inward = (c + 1 - 2 * flip) % 4
    outward = (c + 3 + 2 * flip) % 4
    zhalf = jnp.where(role == 3, core, 1 - core)

    def blk(b):
        return b + flip * (3 - 2 * b)

    own_in = pltpu.make_async_copy(p_ref, arow.at[c], in_s.at[0])
    own_in.start()
    own_b = pltpu.make_async_copy(p_ref, bcol.at[r], in_s.at[1])
    own_b.start()
    pat_in = pltpu.make_async_copy(pat_hbm, pat_ref, in_s.at[2])
    pat_in.start()

    barrier = pltpu.get_barrier_semaphore()
    for d in range(1, 8):
        pl.semaphore_signal(barrier, inc=1, device_id=((r + d) % 8, c), device_id_type=MESH)
    for d in range(1, 4):
        pl.semaphore_signal(barrier, inc=1, device_id=(r, (c + d) % 4), device_id_type=MESH)
    pl.semaphore_wait(barrier, 10)

    def send(src, dst, ss, rs, dev):
        return pltpu.make_async_remote_copy(
            src_ref=src, dst_ref=dst, send_sem=ss, recv_sem=rs, device_id=dev, device_id_type=MESH
        )

    def got(ref, sem):
        send(ref, ref, sem, sem, (sib, c)).wait_recv()

    def start(t):
        t.start()

    def drain(t):
        t.wait_send()

    def piece(k):
        return pl.ds(k * ch, ch) if isinstance(k, int) else pl.ds(pl.multiple_of(k * ch, ch), ch)

    def lane(h):
        return pl.ds(pl.multiple_of(h * half, half), half)

    def inn(k):
        return send(p_ref.at[piece(k)], arow.at[c, piece(k)], inn_s.at[k], inn_r.at[k], (r, inward))

    def mid(pos):
        src = p_ref if pos < NCH else arow.at[blk(0)]
        slot = blk(1) if pos < NCH else blk(0)
        k = pos % NCH
        return send(src.at[piece(k)], arow.at[slot, piece(k)], mid_s.at[pos], mid_r.at[pos], (r, inward))

    def edge(d, k, act):
        pos = (d - 1) * NCH + k
        src = p_ref if d == 1 else arow.at[blk(d)]

        @pl.when(role == d)
        def _():
            act(send(src.at[piece(k)], arow.at[blk(d), piece(k)],
                     edge_s.at[pos], edge_r.at[pos], (r, outward)))

        @pl.when((role != d) & (role != 0))
        def _():
            act(send(src.at[piece(k), lane(zhalf)], arow.at[blk(d), piece(k), lane(zhalf)],
                     edge_s.at[pos], edge_r.at[pos], (r, outward)))

    def edge_got(d, k):
        pos = (d - 1) * NCH + k

        @pl.when(role == d)
        def _():
            got(arow.at[blk(d), piece(k)], edge_r.at[pos])

        @pl.when((role != d) & (role != 0))
        def _():
            got(arow.at[blk(d), piece(k), lane(zhalf)], edge_r.at[pos])

        if d < 3:
            @pl.when(role == 3)
            def _():
                share_far(d, k).start()
        else:
            @pl.when(role == 1)
            def _():
                share_near(1, k).start()

            @pl.when(role == 2)
            def _():
                share_near(2, k).start()

    def share_far(d, k):
        sem = (fa_s if d == 1 else fb_s).at[k]
        return send(arow.at[blk(d), piece(k), lane(zhalf)], xb.at[piece(k)], sem, xb_r.at[k],
                    (yn if d == 1 else xn, c))

    def share_near(me, k):
        dst, sem = (xa, xa_r) if me == 1 else (xb, xb_r)
        to = (yn if me == 1 else xn) + 1 - 2 * core
        return send(arow.at[blk(3), piece(k), lane(zhalf)], dst.at[piece(k)], fa_s.at[k], sem.at[k], (to, c))

    def dia(k):
        return send(bcol.at[yn, piece(k), lane(core)], xa.at[piece(k)], dia_s.at[k], xa_r.at[k], (r, outward))

    def dia_x(k):
        return send(xa.at[piece(k)], xa.at[piece(k)], fa_s.at[k], xa_r.at[k], (xn, c))

    def dia_y(k):
        return send(xa.at[piece(k)], xa.at[piece(k)], fb_s.at[k], xa_r.at[k], (yn, c))

    def x_own(k):
        return send(p_ref.at[piece(k)], bcol.at[r, piece(k)], x_s.at[k], x_r.at[k], (xn, c))

    def y_own(k):
        return send(p_ref.at[piece(k)], bcol.at[r, piece(k)], y_s.at[k], y_r.at[k], (yn, c))

    def y_fwd(k):
        return send(bcol.at[xn, piece(k)], bcol.at[xn, piece(k)], y_s.at[NCH + k], y_r.at[NCH + k], (yn, c))

    def x_fwd(k):
        return send(bcol.at[yn, piece(k)], bcol.at[yn, piece(k)], x_s.at[HALF + k], x_r.at[HALF + k], (xn, c))

    def sib_fwd(slot, k, pos, own=False):
        src = p_ref if own else bcol.at[slot]
        return send(src.at[piece(k)], bcol.at[slot, piece(k)], s_s.at[pos], s_r.at[pos], (sib, c))

    for k in range(NCH):
        @pl.when(is_end)
        def _(k=k):
            inn(k).start()

        @pl.when(is_mid)
        def _(k=k):
            mid(k).start()
            edge(1, k, start)

        x_own(k).start()
        y_own((k + HALF) % NCH).start()
    for k in range(NCH):
        sib_fwd(r, k, k, True).start()

    def part(i, carry):
        tpp, tcc = carry
        at = pl.multiple_of(i * 64, 64)
        w = arow[c, pl.ds(at, 64), :].astype(jnp.float32)
        gr = lax.broadcasted_iota(jnp.int32, w.shape, 0) + (r * rows + at)
        gc = lax.broadcasted_iota(jnp.int32, w.shape, 1) + c * cols
        dpart = jnp.where(gr == gc, w, 0.0)
        return tpp + jnp.sum(dpart, axis=0, keepdims=True), tcc + jnp.sum(w * w, axis=0, keepdims=True)

    own_in.wait()
    own_b.wait()
    pat_in.wait()
    zero = jnp.zeros((1, cols), jnp.float32)
    tpp, tcc = lax.fori_loop(0, rows // 64, part, (zero, zero))
    which = lax.broadcasted_iota(jnp.int32, (8, 128), 0)
    tz[c] = jnp.where(which == 0, jnp.sum(tpp), jnp.sum(tcc))
    tz_out = [send(tz.at[c], tz.at[c], tz_s.at[d], tz_r.at[d], (r, (c + d) % 4)) for d in range(1, 4)]
    for t in tz_out:
        t.start()
    tp_out = [send(tp.at[r], tp.at[r], tp_s.at[d], tp_r.at[d], ((r + d) % 8, c)) for d in range(1, 8)]

    def mid_step(i):
        if i < NCH:
            got(arow.at[blk(0), piece(i)], inn_r.at[i])
            mid(NCH + i).start()
        b = 2 + i // NCH
        got(arow.at[blk(b), piece(i % NCH)], mid_r.at[i])
        edge(b, i % NCH, start)

    for i in range(NCH + HALF):
        @pl.when(is_mid)
        def _():
            mid_step(i)

        @pl.when(is_end)
        def _():
            edge_got(1 + i // NCH, i % NCH)

        if i < NCH:
            kx, ky = i, (i + HALF) % NCH
            got(bcol.at[xn, piece(kx)], x_r.at[kx])
            if kx < HALF:
                y_fwd(kx).start()
            sib_fwd(xn, kx, NCH + kx).start()
            got(bcol.at[yn, piece(ky)], y_r.at[ky])
            if ky >= HALF:
                x_fwd(ky).start()
            sib_fwd(yn, ky, 2 * NCH + ky).start()

            @pl.when(is_mid & (role == 0))
            def _():
                dia(ky).start()
        else:
            k = i - NCH
            got(bcol.at[dg, piece(HALF + k)], x_r.at[NCH + k])
            sib_fwd(dg, HALF + k, 3 * NCH + HALF + k).start()
            got(bcol.at[dg, piece(k)], y_r.at[NCH + k])
            sib_fwd(dg, k, 3 * NCH + k).start()

        if i >= 1 and i <= NCH:
            kd = (i - 1 + HALF) % NCH

            @pl.when(is_end & (role == 0))
            def _():
                got(xa.at[piece(kd)], xa_r.at[kd])
                dia_x(kd).start()
                dia_y(kd).start()

    def traces():
        for d in range(1, 4):
            got(tz.at[(c + 4 - d) % 4], tz_r.at[d])
        tp[r] = ((tz[0] + tz[1]) + tz[2]) + tz[3]
        for t in tp_out:
            t.start()

    sx, sy, sd = xn + 1 - 2 * core, yn + 1 - 2 * core, dg + 1 - 2 * core
    for slot, base in ((sib, 0), (sx, NCH), (sy, 2 * NCH), (sd, 3 * NCH)):
        for k in range(NCH):
            got(bcol.at[slot, piece(k)], s_r.at[base + k])

    def mm(b, h, first=False, only=None):
        slot = blk(b)

        def some(k, _):
            rr = pl.ds(k * mrows, mrows) if isinstance(k, int) else pl.ds(pl.multiple_of(k * mrows, mrows), mrows)
            v = jnp.dot(arow[slot, rr, lane(h)], bcol[2 * slot + h], preferred_element_type=jnp.float32)
            acc[rr, :] = v if first else acc[rr, :] + v
            return 0

        if only is None:
            lax.fori_loop(0, rows // mrows, some, 0)
        else:
            some(only, 0)

    def totals():
        for d in range(1, 8):
            got(tp.at[(r + 8 - d) % 8], tp_r.at[d])
        tot = tp[0]
        for d in range(1, 8):
            tot = tot + tp[d]
        tsum[...] = tot
        sel = lax.broadcasted_iota(jnp.int32, (8, 128), 1) == 0
        trace_p = jnp.sum(jnp.where(sel & (which == 0), tot, 0.0))
        trace_c = jnp.sum(jnp.where(sel & (which == 1), tot, 0.0))
        take = trace_p > 1.0 * order_total
        occ_ref[0] = trace_p / order_total
        occ_ref[1] = jnp.where(take, trace_c, 2.0 * trace_p - trace_c) / order_total

    def mm_all(b):
        lax.fori_loop(0, 2, lambda h, _: (mm(b, h), 0)[1], 0)

    def turn(src, b, h):
        for k in range(NCH):
            arow[blk(b), :, pl.ds(pl.multiple_of(h * half + k * ch, ch), ch)] = src(k).T

    nbr, nbc = pat_ref.shape
    spread = (lax.broadcasted_iota(jnp.int32, (nbc, cols), 1) // BLK
              == lax.broadcasted_iota(jnp.int32, (nbc, cols), 0)).astype(jnp.float32)
    mask[...] = jnp.dot(pat_ref[...].astype(jnp.float32), spread, preferred_element_type=jnp.float32)

    @pl.when(is_mid)
    def _():
        for i in range(NCH + HALF, 2 * NCH - 1):
            mid_step(i)
        mm(1, 0, True)
        mm(1, 1)
        mm_all(0)
        traces()
        mid_step(2 * NCH - 1)
        totals()
        mm_all(2)
        mm_all(3)

    @pl.when(is_end)
    def _():
        mm(0, 0, True)
        mm(0, 1)
        for k in range(HALF, NCH):
            edge_got(2, k)
        traces()

        @pl.when(role == 0)
        def _():
            def slab(t, _):
                b, h = 1 + t // 2, t % 2
                turn(lambda k: bcol[2 * blk(b) + h, piece(k), lane(core)], b, h)
                mm(b, h)
                return 0

            lax.fori_loop(0, 6, slab, 0)
            totals()

        def all_xa():
            for k in range(NCH):
                got(xa.at[piece(k)], xa_r.at[k])

        def all_xb():
            for k in range(NCH):
                got(xb.at[piece(k)], xb_r.at[k])

        other = 1 - zhalf

        @pl.when(role == 1)
        def _():
            all_xa()
            turn(lambda k: xa[piece(k), :], 2, other)
            all_xb()
            turn(lambda k: xb[piece(k), :], 3, other)

        @pl.when(role == 2)
        def _():
            all_xa()
            arow[blk(1), :, lane(other)] = xa[...]
            all_xb()
            turn(lambda k: xb[piece(k), :], 3, other)

        per = mrows // ch

        @pl.when((role == 1) | (role == 2))
        def _():
            mm_all(1)
            mm(3, other)
            for k in range(HALF):
                edge_got(3, k)
            mm(2, 0)
            for k in range(HALF, NCH - 1):
                edge_got(3, k)
            mm(2, 1)
            totals()
            for k in range(3):
                mm(3, zhalf, only=k)
            edge_got(3, NCH - 1)
            mm(3, zhalf, only=3)

        def mm_part(b, h, src, sem, g):
            deep = half // 2
            for k in range(g * HALF, (g + 1) * HALF):
                got(src.at[piece(k)], sem.at[k])
            v = src[pl.ds(g * deep, deep), :].T
            slot = blk(b)
            depth = pl.ds(g * deep, deep)

            for m in range(rows // mrows):
                rr = pl.ds(m * mrows, mrows)
                acc[rr, :] += jnp.dot(v[m * mrows:(m + 1) * mrows, :], bcol[2 * slot + h, depth, :],
                                      preferred_element_type=jnp.float32)

        @pl.when(role == 3)
        def _():
            mm(1, zhalf)
            mm(2, zhalf)
            for k in range(NCH):
                edge_got(3, k)
                if (k + 1) % per == 0:
                    mm(3, 0, only=k // per)
                    mm(3, 1, only=k // per)
                if k == NCH - 2:
                    mm_part(1, other, xa, xa_r, 0)
                    mm_part(2, other, xb, xb_r, 0)
                    totals()
            mm_part(1, other, xa, xa_r, 1)
            mm_part(2, other, xb, xb_r, 1)

    takev = tsum[0:1, 0:1] > 1.0 * order_total
    for b in range(nbr):
        rr = pl.ds(b * BLK, BLK)
        m = mask[b:b + 1, :]
        sq = acc[rr, :] * m
        alt = m * (2.0 * arow[c, rr, :].astype(jnp.float32) - sq)
        out_ref[rr, :] = jnp.where(takev, sq, alt).astype(jnp.bfloat16)

    for t in tz_out + tp_out:
        t.wait_send()
    for k in range(NCH):
        x_own(k).wait_send()
        y_own(k).wait_send()
    for k in range(HALF):
        y_fwd(k).wait_send()
        x_fwd(HALF + k).wait_send()
    for pos in range(4 * NCH):
        sib_fwd(r, 0, pos, True).wait_send()

    @pl.when(is_mid)
    def _():
        for pos in range(2 * NCH):
            mid(pos).wait_send()
        for d in range(1, 4):
            for k in range(NCH):
                edge(d, k, drain)

        @pl.when(role == 0)
        def _():
            for k in range(NCH):
                dia(k).wait_send()

    @pl.when(is_end)
    def _():
        for k in range(NCH):
            inn(k).wait_send()

        @pl.when(role == 0)
        def _():
            for k in range(NCH):
                dia_x(k).wait_send()
                dia_y(k).wait_send()

        @pl.when(role == 3)
        def _():
            for k in range(NCH):
                share_far(1, k).wait_send()
                share_far(2, k).wait_send()

        @pl.when((role == 1) | (role == 2))
        def _():
            for k in range(NCH):
                share_near(1, k).wait_send()


def body(density, pattern):
    rows, cols = density.shape
    order_total = rows * lax.axis_size("row")
    dma = pltpu.SemaphoreType.DMA
    return pl.pallas_call(
        functools.partial(kernel, order_total),
        out_shape=(jax.ShapeDtypeStruct((rows, cols), jnp.bfloat16),
                   jax.ShapeDtypeStruct((2,), jnp.float32)),
        in_specs=[pl.BlockSpec(memory_space=pltpu.HBM)] * 2,
        out_specs=(pl.BlockSpec(memory_space=pltpu.VMEM), pl.BlockSpec(memory_space=pltpu.SMEM)),
        scratch_shapes=[
            pltpu.VMEM((4, rows, cols), jnp.bfloat16),
            pltpu.VMEM((8, rows, cols), jnp.bfloat16),
            pltpu.VMEM((rows, cols), jnp.float32),
            pltpu.VMEM((rows, cols // 2), jnp.bfloat16),
            pltpu.VMEM((rows, cols // 2), jnp.bfloat16),
            pltpu.VMEM((4, 8, 128), jnp.float32),
            pltpu.VMEM((8, 8, 128), jnp.float32),
            pltpu.VMEM((8, 128), jnp.float32),
            pltpu.VMEM(pattern.shape, jnp.int32),
            pltpu.VMEM((pattern.shape[0], cols), jnp.float32),
            dma((3,)),
            dma((2 * NCH,)), dma((2 * NCH,)), dma((NCH,)), dma((NCH,)), dma((3 * NCH,)), dma((3 * NCH,)),
            dma((NCH,)), dma((NCH,)), dma((NCH,)), dma((NCH,)), dma((NCH,)),
            dma((NCH + HALF,)), dma((NCH + HALF,)), dma((NCH + HALF,)), dma((NCH + HALF,)),
            dma((4 * NCH,)), dma((4 * NCH,)),
            dma((4,)), dma((4,)), dma((8,)), dma((8,)),
        ],
        compiler_params=pltpu.CompilerParams(
            collective_id=0, has_side_effects=True, vmem_limit_bytes=40 * 2**20
        ),
    )(density, pattern)


def solution(mesh):
    placed = (P("row", "col"), P("row", "col"))
    fits = mesh.shape["row"] == 8 and mesh.shape["col"] == 4
    return jax.shard_map(
        body if fits else plain_body, mesh=mesh, in_specs=placed,
        out_specs=(P("row", "col"), P()), check_vma=False
    )
```
